32 devices in a mesh: ctx: 2 (over x), fsdp: 16 (over z, y, core).
Axes of the slice: x: 2, y: 2, z: 4, core: 2. Of those that a mesh axis runs over, the one named last changes fastest.
Arguments:
- hidden_in: bfloat16 [16, 256, 1280], P('fsdp', 'ctx'), may hold values from -8 to 8
- values: bfloat16 [16, 256, 2560], P('fsdp', 'ctx'), may hold values from -6 to 6
- log_decay: float32 [16, 40, 256], P('fsdp', None, 'ctx'), may hold values from -1 to 0, as said below
- doc_lengths: int32 [16, 4], P('fsdp'), may hold values from 1 to 128, 256 in all within a row
- proj_bc: bfloat16 [1280, 256], P('fsdp'), may hold values from -0.15625 to 0.15625
- grad_out: bfloat16 [16, 256, 2560], P('fsdp', 'ctx'), may hold values from -6 to 6
Outputs:
- grad_values: bfloat16 [16, 256, 2560], P('fsdp', 'ctx')
- grad_hidden: bfloat16 [16, 256, 1280], P('fsdp', 'ctx')
- grad_proj: float32 [1280, 256], P('fsdp')
The draws below stay inside these ranges and needn't reach their ends.
Inputs may be any that keep to these rules, and one draw needn't show every extreme that they name: `doc_lengths`: each sequence's 4 document lengths sum to 256; the longest is exactly half of 256. `log_decay`: logarithms of decays, all negative.
All inputs are finite; a program needn't handle non-finite values.
Results may differ from the reference program's by a relative error of at most 0.012.
Values may be sent and summed in bfloat16 or wider, within the bound.
A program may use at most 64 MiB of HBM per device.

```python
import math
import jax
import jax.numpy as jnp
import numpy as np
from jax import lax

WIDTH = 1280
HEAD_SUBSET = 40
STATE = 128
DOCS = 4
TOK_DEV = 128
INNER = 2560
SEQUENCE_TOKENS = 256
SEQUENCE_COUNT = 16


def draw_log_decay(key, part):
    random_subkeys = jax.random.split(key, 7)
    quick_share = 0.5
    is_quick = jax.random.uniform(random_subkeys[0], (SEQUENCE_COUNT, HEAD_SUBSET, 1)) < quick_share
    quick_rate = jax.random.uniform(random_subkeys[1], (SEQUENCE_COUNT, HEAD_SUBSET, 1), minval=1.0 / 50, maxval=1.0 / 30)
    slow_rate = jnp.exp(jax.random.uniform(random_subkeys[2], (SEQUENCE_COUNT, HEAD_SUBSET, 1), minval=math.log(0.1 / SEQUENCE_TOKENS), maxval=math.log(0.5 / SEQUENCE_TOKENS)))
    decay_speed = jnp.where(is_quick, quick_rate, slow_rate)
    block_count = SEQUENCE_TOKENS // TOK_DEV
    machine_multiplier = jnp.exp(jax.random.uniform(random_subkeys[3], (SEQUENCE_COUNT, 1, block_count), minval=math.log(0.5), maxval=math.log(2.0)))
    machine_multiplier = jnp.repeat(machine_multiplier, TOK_DEV, axis=2)
    jaggedness = jax.random.uniform(random_subkeys[4], (SEQUENCE_COUNT, HEAD_SUBSET, SEQUENCE_TOKENS), minval=0.5, maxval=1.5)
    spike_places = jax.random.randint(random_subkeys[5], (SEQUENCE_COUNT, 2), 0, SEQUENCE_TOKENS)
    token_places = jnp.arange(SEQUENCE_TOKENS)
    spike_mask = (token_places[None, :] == spike_places[:, 0:1]) | (token_places[None, :] == spike_places[:, 1:2])
    spike_height = jnp.log(jax.random.uniform(random_subkeys[6], (SEQUENCE_COUNT, HEAD_SUBSET, 1), minval=0.5, maxval=0.8))
    final_output = -decay_speed * machine_multiplier * jaggedness + jnp.where(spike_mask[:, None, :], spike_height, 0.0)
    return final_output.astype(jnp.float32)


def strengthened(result, key, source, target, blocks, factor):
    owner, partner = [(jnp.arange(result.shape[dim]) // (result.shape[dim] // blocks)).reshape([-1 if axis == dim else 1 for axis in range(result.ndim)]) for dim in (source, target)]
    chosen = jax.random.permutation(key, blocks)[partner]
    strong = (owner == chosen) | (owner == (partner + blocks // 2) % blocks)
    return jnp.where(strong, factor * result, result)


def shard_levels(own_key, extent, cuts, smallest, high):
    factor_of, own = 1.0, jax.random.fold_in(own_key, 6)
    for dim, shards_of in cuts:
        heights = jnp.exp(jax.random.uniform(jax.random.fold_in(own, dim), (shards_of,), jnp.float32, smallest / len(cuts), high / len(cuts)))
        factor_of = factor_of * jnp.repeat(heights, extent[dim] // shards_of).reshape([-1 if axis == dim else 1 for axis in range(len(extent))])
    return factor_of


def length_profile(amount, total, reach, slope):
    weights = [(1 << 20) // math.isqrt(grade ** slope) + 1 for grade in range(2, amount + 1)]
    surplus, counts = total - reach - (amount - 1), [1] * (amount - 1)
    while surplus > 0:
        candidates = [i for i in range(amount - 1) if counts[i] < reach]
        whole, left = sum([weights[i] for i in candidates]), surplus
        for i in candidates:
            more = min(reach - counts[i], max(1, left * weights[i] // whole), surplus)
            counts[i] = counts[i] + more
            surplus = surplus - more
    return np.array([reach] + counts)


def ragged_sizes(stream_key, amount, total, bound, lean):
    if amount == 2:
        one = jax.random.randint(stream_key, (), max(1, total - bound), min(bound, total - 1) + 1)
        return jnp.stack([one, total - one])
    sizes = jnp.asarray(length_profile(amount, total, bound, lean), jnp.int32)
    couples = (amount - 1) // 2
    source_of, receiver = sizes[1:1 + 2 * couples:2], sizes[2:2 + 2 * couples:2]
    slack = jnp.minimum(source_of - 1, bound - receiver)
    shifted = jax.random.randint(jax.random.fold_in(stream_key, 1), (couples,), 0, 1 << 20) % (slack + 1)
    sizes = sizes.at[1:1 + 2 * couples:2].set(source_of - shifted).at[2:2 + 2 * couples:2].set(receiver + shifted)
    return sizes[jax.random.permutation(jax.random.fold_in(stream_key, 2), amount)]


def scatter_about(key, extent, scale, most, pieces=(), kind=jnp.bfloat16):
    entries = scale * jax.random.normal(key, extent, jnp.float32)
    if pieces:
        entries = entries * shard_levels(key, extent, pieces, -0.22, 0.18)
    return jnp.clip(entries, -most, most).astype(kind)


def bell_draw_with(key, shape, scale, reach, pieces, heavy, kind=jnp.bfloat16):
    values = scale * jax.random.normal(key, shape, jnp.float32)
    if pieces:
        values = values * shard_levels(key, shape, pieces, -0.22, 0.18)
    return jnp.clip(strengthened(values, jax.random.fold_in(key, 3), *heavy), -reach, reach).astype(kind)


def setup_inputs(seed: int = 0) -> dict:
    key_list = jax.random.split(jax.random.key(seed), 7)
    return {
        "hidden_in": bell_draw_with(key_list[0], (SEQUENCE_COUNT, SEQUENCE_TOKENS, WIDTH), 1.0, 8.0, ((0, 16), (1, 2)), (0, 2, 16, 2.0)),
        "values": scatter_about(key_list[1], (SEQUENCE_COUNT, SEQUENCE_TOKENS, INNER), 1.0, 6.0, ((0, 16), (1, 2))),
        "log_decay": draw_log_decay(jax.random.fold_in(key_list[6], 71), 0),
        "doc_lengths": jax.vmap(lambda own: ragged_sizes(own, DOCS, SEQUENCE_TOKENS, SEQUENCE_TOKENS // 2, 1))(jax.random.split(key_list[3], SEQUENCE_COUNT)).reshape((SEQUENCE_COUNT, DOCS)).astype(jnp.int32),
        "proj_bc": scatter_about(key_list[4], (WIDTH, 2 * STATE), WIDTH ** -0.5, 0.15625, ((0, 16),)),
        "grad_out": scatter_about(key_list[5], (SEQUENCE_COUNT, SEQUENCE_TOKENS, INNER), 1.0, 6.0, ((0, 16), (1, 2))),
    }


def combine_pairs(first_pair, second_pair):
    first_decay, first_state = first_pair
    second_decay, second_state = second_pair
    rows_count = first_state.shape[0]
    head_count = first_decay.shape[0]
    decayed = (first_state.reshape(rows_count, head_count, -1) * second_decay[None, :, None]).reshape(first_state.shape)
    return (first_decay * second_decay, decayed + second_state)


def block_terms(b_rows, c_rows, value_rows, grad_rows, decay_rows, doc_ids, prev_doc):
    token_count, state_size = b_rows.shape
    head_count = decay_rows.shape[0]
    inner_width = value_rows.shape[1]
    head_dim = inner_width // head_count
    highest = lax.Precision.HIGHEST
    cumulative = jnp.cumsum(decay_rows, axis=1)
    last_doc = doc_ids[-1]
    token_places = jnp.arange(token_count, dtype=jnp.int32)
    allowed = (doc_ids[:, None] == doc_ids[None, :]) & (token_places[:, None] >= token_places[None, :])
    spread = cumulative[:, :, None] - cumulative[:, None, :]
    decay_matrix = jnp.where(allowed[None], jnp.exp(jnp.where(allowed[None], spread, 0.0)), 0.0)
    in_weight = jnp.exp(cumulative) * (doc_ids == prev_doc).astype(jnp.float32)[None, :]
    out_weight = jnp.exp(cumulative[:, -1:] - cumulative) * (doc_ids == last_doc).astype(jnp.float32)[None, :]
    total_decay = jnp.exp(cumulative[:, -1]) * (last_doc == prev_doc).astype(jnp.float32)
    scores = jnp.dot(c_rows, b_rows.T, preferred_element_type=jnp.float32) / state_size
    mixing = (decay_matrix * scores[None]).astype(jnp.bfloat16)
    value_heads = value_rows.reshape(token_count, head_count, head_dim)
    grad_heads = grad_rows.reshape(token_count, head_count, head_dim)
    products = jnp.einsum("rhp,thp->hrt", grad_heads.astype(jnp.float32), value_heads.astype(jnp.float32), precision=highest)
    kernel = (jnp.sum(decay_matrix * products, axis=0) / state_size).astype(jnp.bfloat16)
    grad_value_local = jnp.einsum("hrt,rhp->thp", mixing.astype(jnp.float32), grad_heads.astype(jnp.float32), precision=highest).reshape(token_count, inner_width)
    grad_b_local = jnp.dot(kernel.T, c_rows, preferred_element_type=jnp.float32)
    grad_c_local = jnp.dot(kernel, b_rows, preferred_element_type=jnp.float32)
    weighted_values = (out_weight.T[:, :, None] * value_heads.astype(jnp.float32)).reshape(token_count, inner_width).astype(jnp.bfloat16)
    weighted_grads = (in_weight.T[:, :, None] * grad_heads.astype(jnp.float32)).reshape(token_count, inner_width).astype(jnp.bfloat16)
    local_state = jnp.dot(b_rows.T, weighted_values, preferred_element_type=jnp.float32)
    local_grad = jnp.dot(c_rows.T, weighted_grads, preferred_element_type=jnp.float32) / state_size
    return (total_decay, local_state, local_grad, out_weight, weighted_values, weighted_grads, grad_value_local, grad_b_local, grad_c_local)


def block_finish(b_rows, terms, state_in, grad_after):
    out_weight = terms[3]
    weighted_values = terms[4]
    weighted_grads = terms[5]
    grad_value_local = terms[6]
    grad_b_local = terms[7]
    grad_c_local = terms[8]
    token_count, state_size = b_rows.shape
    head_count = out_weight.shape[0]
    inner_width = weighted_values.shape[1]
    state_used = state_in.astype(jnp.bfloat16)
    grad_used = grad_after.astype(jnp.bfloat16)
    contract_last = (((1,), (1,)), ((), ()))
    grad_c_edge = lax.dot_general(weighted_grads, state_used, contract_last, preferred_element_type=jnp.float32) / state_size
    grad_b_edge = lax.dot_general(weighted_values, grad_used, contract_last, preferred_element_type=jnp.float32)
    edge_values = jnp.dot(b_rows, grad_used, preferred_element_type=jnp.float32).reshape(token_count, head_count, -1)
    grad_value_edge = (out_weight.T[:, :, None] * edge_values).reshape(token_count, inner_width)
    grad_values = (grad_value_local + grad_value_edge).astype(jnp.bfloat16)
    grad_bc = jnp.concatenate([grad_b_local + grad_b_edge, grad_c_local + grad_c_edge], axis=1).astype(jnp.bfloat16)
    return grad_values, grad_bc


def one_sequence(hidden_rows, value_rows, decay_rows, lengths, grad_rows, proj_bc):
    seq_len = hidden_rows.shape[0]
    block_count = seq_len // TOK_DEV
    projected = jnp.dot(hidden_rows, proj_bc, preferred_element_type=jnp.float32).astype(jnp.bfloat16)
    b_rows = projected[:, :STATE]
    c_rows = projected[:, STATE:]
    doc_starts = jnp.cumsum(lengths) - lengths
    token_places = jnp.arange(seq_len, dtype=jnp.int32)
    doc_ids = jnp.sum((doc_starts[None, :] <= token_places[:, None]).astype(jnp.int32), axis=1)
    prev_docs = jnp.concatenate([jnp.zeros((1,), jnp.int32), doc_ids[TOK_DEV - 1::TOK_DEV][:-1]])

    def to_blocks(array):
        return array.reshape(block_count, TOK_DEV, -1)

    decay_blocks = decay_rows.reshape(HEAD_SUBSET, block_count, TOK_DEV).transpose(1, 0, 2)
    terms = jax.vmap(block_terms)(to_blocks(b_rows), to_blocks(c_rows), to_blocks(value_rows), to_blocks(grad_rows), decay_blocks, doc_ids.reshape(block_count, TOK_DEV), prev_docs)
    identity_decay = jnp.ones((HEAD_SUBSET,), jnp.float32)

    def chain_step(running, pair):
        return combine_pairs((identity_decay, running), pair)[1], running

    zero_state = jnp.zeros(terms[1].shape[1:], jnp.float32)
    final_state, states_in = lax.scan(chain_step, zero_state, (terms[0], terms[1]))
    final_grad, grads_after = lax.scan(chain_step, zero_state, (terms[0], terms[2]), reverse=True)
    grad_values, grad_bc = jax.vmap(block_finish)(to_blocks(b_rows), terms, states_in, grads_after)
    grad_values = grad_values.reshape(seq_len, -1)
    grad_bc = grad_bc.reshape(seq_len, -1)
    grad_hidden = lax.dot_general(grad_bc, proj_bc, (((1,), (1,)), ((), ())), preferred_element_type=jnp.float32).astype(jnp.bfloat16)
    return grad_values, grad_hidden, grad_bc


def reference(hidden_in, values, log_decay, doc_lengths, proj_bc, grad_out):
    def per_sequence(sequence_items):
        hidden_rows, value_rows, decay_rows, lengths, grad_rows = sequence_items
        return one_sequence(hidden_rows, value_rows, decay_rows, lengths, grad_rows, proj_bc)

    grad_values, grad_hidden, grad_bc = lax.map(per_sequence, (hidden_in, values, log_decay, doc_lengths, grad_out))
    grad_proj = lax.dot_general(hidden_in.reshape(-1, WIDTH), grad_bc.reshape(-1, 2 * STATE), (((0,), (0,)), ((), ())), preferred_element_type=jnp.float32) / SEQUENCE_COUNT
    return grad_values, grad_hidden, grad_proj
```

```python
import functools

import jax
import jax.numpy as jnp
from jax import lax
from jax.experimental import pallas as pl
from jax.experimental.pallas import tpu as pltpu
from jax.sharding import PartitionSpec as P

F32 = jnp.float32
BF16 = jnp.bfloat16
NN = (((1,), (0,)), ((), ()))
NT = (((1,), (1,)), ((), ()))
VM = pl.BlockSpec(memory_space=pltpu.VMEM)
SM = pl.BlockSpec(memory_space=pltpu.SMEM)


def mm(a, b, dims=NN):
    return lax.dot_general(a, b, dims, preferred_element_type=F32)


def send(src, dst, s, r, device):
    return pltpu.make_async_remote_copy(
        src_ref=src,
        dst_ref=dst,
        send_sem=s,
        recv_sem=r,
        device_id=device,
        device_id_type=pl.DeviceIdType.MESH,
    )


def greet(devices):
    barrier = pltpu.get_barrier_semaphore()
    for device in devices:
        pl.semaphore_signal(
            barrier, inc=1, device_id=device, device_id_type=pl.DeviceIdType.MESH
        )
    pl.semaphore_wait(barrier, len(devices))


def gather_kernel(n, x_ref, o_ref, s1, r1, s2, r2, own_sem):
    me = lax.axis_index("fsdp")
    half = n // 2
    mate = {"fsdp": me + 1 - 2 * (me % 2)}
    peers = [{"fsdp": (me + 2 * k) % n} for k in range(1, half)]
    greet([mate] + peers)
    own = pltpu.make_async_copy(x_ref, o_ref.at[me], own_sem)
    own.start()
    first = [send(x_ref, o_ref.at[me], s1.at[k], r1.at[k], p) for k, p in enumerate(peers)]
    for copy in first:
        copy.start()
    second = [send(x_ref, o_ref.at[me], s2.at[0], r2.at[0], mate)]
    second[0].start()
    for k in range(1, half):
        block = o_ref.at[(me + n - 2 * k) % n]
        send(x_ref, block, s1.at[k - 1], r1.at[k - 1], peers[k - 1]).wait_recv()
        second.append(send(block, block, s2.at[k], r2.at[k], mate))
        second[k].start()
    own.wait()
    for copy in first:
        copy.wait_send()
    for k in range(half):
        second[k].wait_send()
        block = o_ref.at[(mate["fsdp"] + n - 2 * k) % n]
        send(x_ref, block, s2.at[k], r2.at[k], mate).wait_recv()


def gather(shard, n):
    sems = [pltpu.SemaphoreType.DMA((n // 2,))] * 4 + [pltpu.SemaphoreType.DMA]
    whole = pl.pallas_call(
        functools.partial(gather_kernel, n),
        out_shape=jax.ShapeDtypeStruct((n,) + shard.shape, shard.dtype),
        in_specs=[VM],
        out_specs=VM,
        scratch_shapes=sems,
        compiler_params=pltpu.CompilerParams(collective_id=0, has_side_effects=True),
        name="gather_proj",
    )(shard)
    return whole.reshape(-1, shard.shape[1])


def scatter_kernel(n, x_ref, o_ref, a_ref, y_ref, z_ref, w_ref, u_ref, s1, r1, s2, r2, s3, r3):
    me = lax.axis_index("fsdp")
    half = n // 2
    par = me % 2
    mine = me // 2
    mate = {"fsdp": me + 1 - 2 * par}
    across = {"ctx": 1 - lax.axis_index("ctx")}
    spots = [(mine + k + 1) % half for k in range(half)]
    peers = [{"fsdp": 2 * j + par} for j in spots[:-1]]
    greet([mate, across] + peers)
    first = [
        send(x_ref.at[j, 1 - par], a_ref.at[k], s1.at[k], r1.at[k], mate)
        for k, j in enumerate(spots)
    ]
    for copy in first:
        copy.start()
    second = []
    for k in range(half - 1):
        first[k].wait_recv()
        y_ref[k] = (x_ref[spots[k], par].astype(F32) + a_ref[k].astype(F32)).astype(BF16)
        second.append(send(y_ref.at[k], z_ref.at[k], s2.at[k], r2.at[k], peers[k]))
        second[k].start()
    first[half - 1].wait_recv()
    total = x_ref[mine, par].astype(F32) + a_ref[half - 1].astype(F32)
    for copy in first:
        copy.wait_send()
    for k in range(half - 1):
        second[k].wait()
        total = total + z_ref[k].astype(F32)
    w_ref[...] = total
    last = send(w_ref, u_ref, s3, r3, across)
    last.start()
    last.wait()
    o_ref[...] = w_ref[...] + u_ref[...]


def scatter_sum(term, n):
    rows, cols = term.shape[0] // n, term.shape[1]
    half = n // 2
    return pl.pallas_call(
        functools.partial(scatter_kernel, n),
        out_shape=jax.ShapeDtypeStruct((rows, cols), F32),
        in_specs=[VM],
        out_specs=VM,
        scratch_shapes=[pltpu.VMEM((half, rows, cols), BF16)] * 3
        + [pltpu.VMEM((rows, cols), F32)] * 2
        + [pltpu.SemaphoreType.DMA((half,))] * 4
        + [pltpu.SemaphoreType.DMA] * 2,
        compiler_params=pltpu.CompilerParams(collective_id=1, has_side_effects=True),
        name="scatter_proj",
    )(term.reshape(half, 2, rows, cols))


def doc_of(lengths_ref, places):
    start, count = jnp.int32(0), jnp.zeros(places.shape, jnp.int32)
    for k in range(lengths_ref.shape[1]):
        count = count + (start <= places).astype(jnp.int32)
        start = start + lengths_ref[0, k]
    return count


def prefix_sums(decay_ref):
    tokens = decay_ref.shape[1]
    r = lax.broadcasted_iota(jnp.int32, (tokens, tokens), 0)
    t = lax.broadcasted_iota(jnp.int32, (tokens, tokens), 1)
    exact = functools.partial(
        lax.dot_general, precision=lax.Precision.HIGHEST, preferred_element_type=F32
    )
    rows = exact(decay_ref[...], (r <= t).astype(F32), NN)
    columns = exact((r >= t).astype(F32), decay_ref[...], NT)
    return rows, columns


def spread_pair(weights, h, low):
    return jnp.where(low, weights[:, h : h + 1], weights[:, h + 1 : h + 2])


def out_weights(columns, lengths_ref, first_token):
    tokens = columns.shape[0]
    places = lax.broadcasted_iota(jnp.int32, columns.shape, 0) + first_token
    docs = doc_of(lengths_ref, places)
    last = doc_of(lengths_ref, jnp.full(columns.shape, first_token + tokens - 1, jnp.int32))
    return docs, jnp.where(docs == last, jnp.exp(columns[tokens - 1 :, :] - columns), 0.0)


def start_kernel(len_ref, hid_ref, proj_ref, val_ref, grad_ref, dec_ref, bc_ref, pay_ref, sel_ref):
    tokens, state = hid_ref.shape[0], proj_ref.shape[1] // 2
    lead = lax.axis_index("ctx") == 0
    first_token = lax.axis_index("ctx") * tokens
    bc = mm(hid_ref[...], proj_ref[...]).astype(BF16)
    bc_ref[...] = bc
    _, columns = prefix_sums(dec_ref)
    docs, out_w = out_weights(columns, len_ref, first_token)
    prev = doc_of(len_ref, jnp.full(columns.shape, first_token - 1, jnp.int32))
    in_w = jnp.where(docs == prev, jnp.exp(columns), 0.0)
    lead_v = jnp.full((tokens, state), lead.astype(jnp.int32), jnp.int32) == 1
    weights = jnp.where(lead_v[:, : columns.shape[1]], out_w, in_w)
    side = jnp.where(lead_v, bc[:, :state].astype(F32), bc[:, state:].astype(F32))
    turned = (side.T).astype(BF16)
    scale = jnp.where(lead, 1.0, 1.0 / state).astype(F32)
    low = lax.broadcasted_iota(jnp.int32, (tokens, 128), 1) < 64
    for p in range(val_ref.shape[1] // 128):
        at = slice(128 * p, 128 * p + 128)
        raw = jnp.where(lead_v, val_ref[:, at].astype(F32), grad_ref[:, at].astype(F32))
        weighted = (raw * spread_pair(weights, 2 * p, low)).astype(BF16)
        sel_ref[:, at] = weighted
        pay_ref[:, at] = (mm(turned, weighted) * scale).astype(BF16)


def middle_kernel(len_ref, bc_ref, val_ref, grad_ref, dec_ref, gv_ref, gbc_ref):
    tokens, state = bc_ref.shape[0], bc_ref.shape[1] // 2
    first_token = lax.axis_index("ctx") * tokens
    rows, columns = prefix_sums(dec_ref)
    t = lax.broadcasted_iota(jnp.int32, (tokens, tokens), 0)
    r = lax.broadcasted_iota(jnp.int32, (tokens, tokens), 1)
    allowed = (doc_of(len_ref, t + first_token) == doc_of(len_ref, r + first_token)) & (r >= t)
    b, c = bc_ref[:, :state], bc_ref[:, state:]
    scores = mm(b, c, NT) / state
    low = lax.broadcasted_iota(jnp.int32, (tokens, 128), 1) < 64
    none = jnp.zeros((tokens, 128), BF16)
    kernel = jnp.zeros((tokens, tokens), F32)
    for p in range(val_ref.shape[1] // 128):
        at = slice(128 * p, 128 * p + 128)
        v, g = val_ref[:, at], grad_ref[:, at]
        split_v = jnp.concatenate([jnp.where(low, v, none), jnp.where(low, none, v)], axis=0)
        split_g = jnp.concatenate([jnp.where(low, g, none), jnp.where(low, none, g)], axis=0)
        products = mm(split_v, g, NT)
        mixes = []
        for i in range(2):
            h = 2 * p + i
            spread = rows[h : h + 1, :] - columns[:, h : h + 1]
            decay = jnp.exp(jnp.where(allowed, spread, -1e30))
            kernel = kernel + decay * products[i * tokens : (i + 1) * tokens, :]
            mixes.append((decay * scores).astype(BF16))
        gv_ref[:, at] = mm(jnp.concatenate(mixes, axis=1), split_g)
    kernel = kernel / state
    gbc_ref[:, :state] = mm(kernel.astype(BF16), c)
    gbc_ref[:, state:] = mm(kernel.T.astype(BF16), b)


def end_kernel(
    seq_total, len_ref, got_ref, sel_ref, gv_ref, gbc_ref, bc_ref, dec_ref, proj_ref, hid_ref,
    out_ref, hidden_ref, term_ref,
):
    tokens, state = bc_ref.shape[0], bc_ref.shape[1] // 2
    lead = (lax.axis_index("ctx") == 0).astype(F32)
    _, columns = prefix_sums(dec_ref)
    _, out_w = out_weights(columns, len_ref, lax.axis_index("ctx") * tokens)
    out_w = out_w * lead
    low = lax.broadcasted_iota(jnp.int32, (tokens, 128), 1) < 64
    edge = mm(sel_ref[...], got_ref[...], NT)
    b = bc_ref[:, :state]
    for p in range(got_ref.shape[1] // 128):
        at = slice(128 * p, 128 * p + 128)
        more = mm(b, got_ref[:, at]) * spread_pair(out_w, 2 * p, low)
        out_ref[:, at] = (gv_ref[:, at] + more).astype(BF16)
    gb = (gbc_ref[:, :state] + edge * lead).astype(BF16)
    gc = (gbc_ref[:, state:] + edge * ((1.0 - lead) / state)).astype(BF16)
    gbc = jnp.concatenate([gb, gc], axis=1)
    hidden_ref[...] = mm(gbc, proj_ref[...], NT).astype(BF16)
    turned = hid_ref[...].astype(F32).T.astype(BF16)
    term_ref[...] = (mm(turned, gbc) / seq_total).astype(BF16)


def call(body, name, flops, outs, *args):
    shapes = tuple(jax.ShapeDtypeStruct(s, d) for s, d in outs)
    return pl.pallas_call(
        body,
        out_shape=shapes,
        in_specs=[SM] + [VM] * (len(args) - 1),
        out_specs=tuple(VM for _ in shapes),
        cost_estimate=pl.CostEstimate(flops=flops, bytes_accessed=4000000, transcendentals=0),
        name=name,
    )(*args)


def paired(hidden_in, values, log_decay, doc_lengths, proj_bc, grad_out):
    n = lax.axis_size("fsdp")
    hid, val, dec, grad = hidden_in[0], values[0], log_decay[0], grad_out[0]
    tokens, inner = val.shape
    wide = proj_bc.shape[1]
    proj = gather(proj_bc, n)
    bc, pay, sel = call(
        start_kernel, "start", 200000000,
        [((tokens, wide), BF16), ((wide // 2, inner), BF16), ((tokens, inner), BF16)],
        doc_lengths, hid, proj, val, grad, dec,
    )
    got = lax.ppermute(pay, "ctx", [(0, 1), (1, 0)])
    gv, gbc = call(
        middle_kernel, "middle", 4000000000,
        [((tokens, inner), F32), ((tokens, wide), F32)],
        doc_lengths, bc, val, grad, dec,
    )
    out, hidden, term = call(
        functools.partial(end_kernel, n * hidden_in.shape[0]), "end", 400000000,
        [((tokens, inner), BF16), (hid.shape, BF16), ((hid.shape[1], wide), BF16)],
        doc_lengths, got, sel, gv, gbc, bc, dec, proj, hid,
    )
    return (out[None], hidden[None], scatter_sum(term, n))


def entering(value, axis, combine, identity, reverse):
    length, mine = (lax.axis_size(axis), lax.axis_index(axis))
    everything = jax.tree.map(
        lambda part, kind: lax.all_gather(part.astype(kind), axis),
        value,
        (jnp.bfloat16, jnp.bfloat16),
    )
    start = jax.tree.map(
        lambda part, zero: jnp.broadcast_to(jnp.asarray(zero, part.dtype), part.shape),
        value,
        identity,
    )

    def turn(k, before):
        at = length - 1 - k if reverse else k
        reached = at > mine if reverse else at < mine
        new = combine(
            before, jax.tree.map(lambda part, own: part[at].astype(own.dtype), everything, value)
        )
        return jax.tree.map(lambda a, b: jnp.where(reached, a, b), new, before)

    return lax.fori_loop(0, length, turn, start)


def combine_pairs(first_pair, second_pair):
    first_decay, first_state = first_pair
    second_decay, second_state = second_pair
    rows_count = first_state.shape[0]
    head_count = first_decay.shape[0]
    decayed = (
        first_state.reshape(rows_count, head_count, -1) * second_decay[None, :, None]
    ).reshape(first_state.shape)
    return (first_decay * second_decay, decayed + second_state)


def block_terms(b_rows, c_rows, value_rows, grad_rows, decay_rows, doc_ids, prev_doc):
    token_count, state_size = b_rows.shape
    head_count = decay_rows.shape[0]
    inner_width = value_rows.shape[1]
    head_dim = inner_width // head_count
    cumulative = jnp.cumsum(decay_rows, axis=1)
    last_doc = doc_ids[-1]
    token_places = jnp.arange(token_count, dtype=jnp.int32)
    allowed = (doc_ids[:, None] == doc_ids[None, :]) & (
        token_places[:, None] >= token_places[None, :]
    )
    spread = cumulative[:, :, None] - cumulative[:, None, :]
    decay_matrix = jnp.where(allowed[None], jnp.exp(jnp.where(allowed[None], spread, 0.0)), 0.0)
    in_weight = jnp.exp(cumulative) * (doc_ids == prev_doc).astype(jnp.float32)[None, :]
    out_weight = (
        jnp.exp(cumulative[:, -1:] - cumulative)
        * (doc_ids == last_doc).astype(jnp.float32)[None, :]
    )
    total_decay = jnp.exp(cumulative[:, -1]) * (last_doc == prev_doc).astype(jnp.float32)
    contract_last = (((1,), (1,)), ((), ()))
    scores = (
        lax.dot_general(c_rows, b_rows, contract_last, preferred_element_type=jnp.float32)
        / state_size
    )
    mixing = (decay_matrix * scores[None]).astype(jnp.bfloat16)
    value_heads = value_rows.reshape(token_count, head_count, head_dim)
    grad_heads = grad_rows.reshape(token_count, head_count, head_dim)
    products = jnp.einsum(
        "rhp,thp->hrt", grad_heads, value_heads, preferred_element_type=jnp.float32
    )
    kernel = (jnp.sum(decay_matrix * products, axis=0) / state_size).astype(jnp.bfloat16)
    grad_value_local = jnp.einsum(
        "hrt,rhp->thp", mixing, grad_heads, preferred_element_type=jnp.float32
    ).reshape(token_count, inner_width)
    contract_first = (((0,), (0,)), ((), ()))
    grad_b_local = lax.dot_general(
        kernel, c_rows, contract_first, preferred_element_type=jnp.float32
    )
    grad_c_local = jnp.dot(kernel, b_rows, preferred_element_type=jnp.float32)
    weighted_values = (
        (out_weight.T[:, :, None] * value_heads)
        .reshape(token_count, inner_width)
        .astype(jnp.bfloat16)
    )
    weighted_grads = (
        (in_weight.T[:, :, None] * grad_heads)
        .reshape(token_count, inner_width)
        .astype(jnp.bfloat16)
    )
    local_state = lax.dot_general(
        b_rows, weighted_values, contract_first, preferred_element_type=jnp.float32
    )
    local_grad = (
        lax.dot_general(c_rows, weighted_grads, contract_first, preferred_element_type=jnp.float32)
        / state_size
    )
    return (
        total_decay,
        local_state,
        local_grad,
        out_weight,
        weighted_values,
        weighted_grads,
        grad_value_local,
        grad_b_local,
        grad_c_local,
    )


def block_finish(b_rows, terms, state_in, grad_after):
    out_weight = terms[3]
    weighted_values = terms[4]
    weighted_grads = terms[5]
    grad_value_local = terms[6]
    grad_b_local = terms[7]
    grad_c_local = terms[8]
    token_count, state_size = b_rows.shape
    head_count = out_weight.shape[0]
    inner_width = weighted_values.shape[1]
    state_used = state_in.astype(jnp.bfloat16)
    grad_used = grad_after.astype(jnp.bfloat16)
    contract_last = (((1,), (1,)), ((), ()))
    grad_c_edge = (
        lax.dot_general(
            weighted_grads, state_used, contract_last, preferred_element_type=jnp.float32
        )
        / state_size
    )
    grad_b_edge = lax.dot_general(
        weighted_values, grad_used, contract_last, preferred_element_type=jnp.float32
    )
    edge_values = jnp.dot(b_rows, grad_used, preferred_element_type=jnp.float32).reshape(
        token_count, head_count, -1
    )
    grad_value_edge = (out_weight.T[:, :, None] * edge_values).reshape(token_count, inner_width)
    grad_values = (grad_value_local + grad_value_edge).astype(jnp.bfloat16)
    grad_bc = jnp.concatenate(
        [grad_b_local + grad_b_edge, grad_c_local + grad_c_edge], axis=1
    ).astype(jnp.bfloat16)
    return (grad_values, grad_bc)


def local(hidden_in, values, log_decay, doc_lengths, proj_bc, grad_out):
    token_count = hidden_in.shape[1]
    state_size = proj_bc.shape[1] // 2
    hidden_rows = hidden_in[0]
    first_proj = lax.all_gather(proj_bc, "fsdp", axis=0, tiled=True)
    projected = jnp.dot(hidden_rows, first_proj, preferred_element_type=jnp.float32).astype(
        jnp.bfloat16
    )
    b_rows = projected[:, :state_size]
    c_rows = projected[:, state_size:]
    lengths = doc_lengths[0]
    doc_starts = jnp.cumsum(lengths) - lengths
    first_token = lax.axis_index("ctx") * token_count
    token_places = first_token + jnp.arange(token_count, dtype=jnp.int32)
    doc_ids = jnp.sum((doc_starts[None, :] <= token_places[:, None]).astype(jnp.int32), axis=1)
    prev_doc = jnp.sum((doc_starts <= first_token - 1).astype(jnp.int32))
    terms = block_terms(b_rows, c_rows, values[0], grad_out[0], log_decay[0], doc_ids, prev_doc)
    total_decay = terms[0]
    unit_pair = (jnp.ones_like(total_decay), jnp.zeros_like(terms[1]))
    state_in = entering((total_decay, terms[1]), "ctx", combine_pairs, unit_pair, False)[1]
    grad_after = entering((total_decay, terms[2]), "ctx", combine_pairs, unit_pair, True)[1]
    grad_values, grad_bc = block_finish(b_rows, terms, state_in, grad_after)
    contract_last = (((1,), (1,)), ((), ()))
    grad_hidden = lax.dot_general(
        grad_bc, first_proj, contract_last, preferred_element_type=jnp.float32
    ).astype(jnp.bfloat16)
    seq_total = lax.axis_size("fsdp") * hidden_in.shape[0]
    contract_first = (((0,), (0,)), ((), ()))
    full_term = (
        lax.dot_general(hidden_rows, grad_bc, contract_first, preferred_element_type=jnp.float32)
        / seq_total
    )
    summed = lax.psum(full_term, "ctx")
    grad_proj = lax.psum_scatter(summed, "fsdp", scatter_dimension=0, tiled=True)
    return (grad_values[None], grad_hidden[None], grad_proj)


def solution(mesh):
    in_specs = (
        P("fsdp", "ctx", None),
        P("fsdp", "ctx", None),
        P("fsdp", None, "ctx"),
        P("fsdp", None),
        P("fsdp", None),
        P("fsdp", "ctx", None),
    )
    out_specs = (P("fsdp", "ctx", None), P("fsdp", "ctx", None), P("fsdp", None))
    body = paired if mesh.shape["ctx"] == 2 and mesh.shape["fsdp"] % 2 == 0 else local
    return jax.shard_map(body, mesh=mesh, in_specs=in_specs, out_specs=out_specs, check_vma=False)
```

```python
import functools

import jax
import jax.numpy as jnp
from jax import lax
from jax.experimental import pallas as pl
from jax.experimental.pallas import tpu as pltpu
from jax.sharding import PartitionSpec as P

F32 = jnp.float32
BF16 = jnp.bfloat16
NN = (((1,), (0,)), ((), ()))
NT = (((1,), (1,)), ((), ()))
VM = pl.BlockSpec(memory_space=pltpu.VMEM)
SM = pl.BlockSpec(memory_space=pltpu.SMEM)


def mm(a, b, dims=NN):
    return lax.dot_general(a, b, dims, preferred_element_type=F32)


def send(src, dst, s, r, device):
    return pltpu.make_async_remote_copy(
        src_ref=src,
        dst_ref=dst,
        send_sem=s,
        recv_sem=r,
        device_id=device,
        device_id_type=pl.DeviceIdType.MESH,
    )


def greet(devices):
    barrier = pltpu.get_barrier_semaphore()
    for device in devices:
        pl.semaphore_signal(
            barrier, inc=1, device_id=device, device_id_type=pl.DeviceIdType.MESH
        )
    pl.semaphore_wait(barrier, len(devices))


def gather_kernel(n, x_ref, o_ref, s1, r1, s2, r2, own_sem):
    me = lax.axis_index("fsdp")
    half = n // 2
    mate = {"fsdp": me + 1 - 2 * (me % 2)}
    peers = [{"fsdp": (me + 2 * k) % n} for k in range(1, half)]
    greet([mate] + peers)
    own = pltpu.make_async_copy(x_ref, o_ref.at[me], own_sem)
    own.start()
    first = [send(x_ref, o_ref.at[me], s1.at[k], r1.at[k], p) for k, p in enumerate(peers)]
    for copy in first:
        copy.start()
    second = [send(x_ref, o_ref.at[me], s2.at[0], r2.at[0], mate)]
    second[0].start()
    for k in range(1, half):
        block = o_ref.at[(me + n - 2 * k) % n]
        send(x_ref, block, s1.at[k - 1], r1.at[k - 1], peers[k - 1]).wait_recv()
        second.append(send(block, block, s2.at[k], r2.at[k], mate))
        second[k].start()
    own.wait()
    for copy in first:
        copy.wait_send()
    for k in range(half):
        second[k].wait_send()
        block = o_ref.at[(mate["fsdp"] + n - 2 * k) % n]
        send(x_ref, block, s2.at[k], r2.at[k], mate).wait_recv()


def gather(shard, n):
    sems = [pltpu.SemaphoreType.DMA((n // 2,))] * 4 + [pltpu.SemaphoreType.DMA]
    whole = pl.pallas_call(
        functools.partial(gather_kernel, n),
        out_shape=jax.ShapeDtypeStruct((n,) + shard.shape, shard.dtype),
        in_specs=[VM],
        out_specs=VM,
        scratch_shapes=sems,
        compiler_params=pltpu.CompilerParams(collective_id=0, has_side_effects=True),
        cost_estimate=pl.CostEstimate(
            flops=15000000000, bytes_accessed=1000000, transcendentals=0
        ),
        name="gather_proj",
    )(shard)
    return whole.reshape(-1, shard.shape[1])


def scatter_kernel(n, x_ref, o_ref, a_ref, y_ref, z_ref, w_ref, u_ref, s1, r1, s2, r2, s3, r3):
    me = lax.axis_index("fsdp")
    half = n // 2
    par = me % 2
    mine = me // 2
    mate = {"fsdp": me + 1 - 2 * par}
    across = {"ctx": 1 - lax.axis_index("ctx")}
    spots = [(mine + k + 1) % half for k in range(half)]
    peers = [{"fsdp": 2 * j + par} for j in spots[:-1]]
    greet([mate, across] + peers)
    first = [
        send(x_ref.at[j, 1 - par], a_ref.at[k], s1.at[k], r1.at[k], mate)
        for k, j in enumerate(spots)
    ]
    for copy in first:
        copy.start()
    second = []
    for k in range(half - 1):
        first[k].wait_recv()
        y_ref[k] = (x_ref[spots[k], par].astype(F32) + a_ref[k].astype(F32)).astype(BF16)
        second.append(send(y_ref.at[k], z_ref.at[k], s2.at[k], r2.at[k], peers[k]))
        second[k].start()
    first[half - 1].wait_recv()
    total = x_ref[mine, par].astype(F32) + a_ref[half - 1].astype(F32)
    for copy in first:
        copy.wait_send()
    for k in range(half - 1):
        second[k].wait()
        total = total + z_ref[k].astype(F32)
    w_ref[...] = total
    last = send(w_ref, u_ref, s3, r3, across)
    last.start()
    last.wait()
    o_ref[...] = w_ref[...] + u_ref[...]


def scatter_sum(term, n):
    rows, cols = term.shape[0] // n, term.shape[1]
    half = n // 2
    return pl.pallas_call(
        functools.partial(scatter_kernel, n),
        out_shape=jax.ShapeDtypeStruct((rows, cols), F32),
        in_specs=[VM],
        out_specs=VM,
        scratch_shapes=[pltpu.VMEM((half, rows, cols), BF16)] * 3
        + [pltpu.VMEM((rows, cols), F32)] * 2
        + [pltpu.SemaphoreType.DMA((half,))] * 4
        + [pltpu.SemaphoreType.DMA] * 2,
        compiler_params=pltpu.CompilerParams(collective_id=1, has_side_effects=True),
        name="scatter_proj",
    )(term.reshape(half, 2, rows, cols))


def doc_of(lengths_ref, places):
    start, count = jnp.int32(0), jnp.zeros(places.shape, jnp.int32)
    for k in range(lengths_ref.shape[1]):
        count = count + (start <= places).astype(jnp.int32)
        start = start + lengths_ref[0, k]
    return count


def prefix_sums(decay_ref):
    tokens = decay_ref.shape[1]
    r = lax.broadcasted_iota(jnp.int32, (tokens, tokens), 0)
    t = lax.broadcasted_iota(jnp.int32, (tokens, tokens), 1)
    exact = functools.partial(
        lax.dot_general, precision=lax.Precision.HIGHEST, preferred_element_type=F32
    )
    rows = exact(decay_ref[...], (r <= t).astype(F32), NN)
    columns = exact((r >= t).astype(F32), decay_ref[...], NT)
    return rows, columns


def spread_pair(weights, h, low):
    return jnp.where(low, weights[:, h : h + 1], weights[:, h + 1 : h + 2])


def out_weights(columns, lengths_ref, first_token):
    tokens = columns.shape[0]
    places = lax.broadcasted_iota(jnp.int32, columns.shape, 0) + first_token
    docs = doc_of(lengths_ref, places)
    last = doc_of(lengths_ref, jnp.full(columns.shape, first_token + tokens - 1, jnp.int32))
    return docs, jnp.where(docs == last, jnp.exp(columns[tokens - 1 :, :] - columns), 0.0)


def weigh_kernel(len_ref, val_ref, grad_ref, dec_ref, sel_ref):
    tokens = val_ref.shape[0]
    lead = lax.axis_index("ctx") == 0
    first_token = lax.axis_index("ctx") * tokens
    _, columns = prefix_sums(dec_ref)
    docs, out_w = out_weights(columns, len_ref, first_token)
    prev = doc_of(len_ref, jnp.full(columns.shape, first_token - 1, jnp.int32))
    in_w = jnp.where(docs == prev, jnp.exp(columns), 0.0)
    lead_v = jnp.full((tokens, 128), lead.astype(jnp.int32), jnp.int32) == 1
    weights = jnp.where(lead_v[:, : columns.shape[1]], out_w, in_w)
    low = lax.broadcasted_iota(jnp.int32, (tokens, 128), 1) < 64
    for p in range(val_ref.shape[1] // 128):
        at = slice(128 * p, 128 * p + 128)
        raw = jnp.where(lead_v, val_ref[:, at].astype(F32), grad_ref[:, at].astype(F32))
        sel_ref[:, at] = (raw * spread_pair(weights, 2 * p, low)).astype(BF16)


def project_kernel(len_ref, hid_ref, proj_ref, bc_ref, side_ref):
    tokens, state = hid_ref.shape[0], proj_ref.shape[1] // 2
    bc = mm(hid_ref[...], proj_ref[...])
    bc_ref[...] = bc.astype(BF16)
    lead_v = jnp.full((tokens, state), 1 - lax.axis_index("ctx"), jnp.int32) == 1
    side = jnp.where(lead_v, bc[:, :state], bc[:, state:])
    side_ref[...] = side.T.astype(BF16)


def middle_kernel(len_ref, bc_ref, val_ref, grad_ref, dec_ref, gv_ref, gbc_ref):
    tokens, state = bc_ref.shape[0], bc_ref.shape[1] // 2
    first_token = lax.axis_index("ctx") * tokens
    rows, columns = prefix_sums(dec_ref)
    t = lax.broadcasted_iota(jnp.int32, (tokens, tokens), 0)
    r = lax.broadcasted_iota(jnp.int32, (tokens, tokens), 1)
    allowed = (doc_of(len_ref, t + first_token) == doc_of(len_ref, r + first_token)) & (r >= t)
    b, c = bc_ref[:, :state], bc_ref[:, state:]
    scores = mm(b, c, NT) / state
    low = lax.broadcasted_iota(jnp.int32, (tokens, 128), 1) < 64
    none = jnp.zeros((tokens, 128), BF16)
    kernel = jnp.zeros((tokens, tokens), F32)
    for p in range(val_ref.shape[1] // 128):
        at = slice(128 * p, 128 * p + 128)
        v, g = val_ref[:, at], grad_ref[:, at]
        split_v = jnp.concatenate([jnp.where(low, v, none), jnp.where(low, none, v)], axis=0)
        split_g = jnp.concatenate([jnp.where(low, g, none), jnp.where(low, none, g)], axis=0)
        products = mm(split_v, g, NT)
        mixes = []
        for i in range(2):
            h = 2 * p + i
            spread = rows[h : h + 1, :] - columns[:, h : h + 1]
            decay = jnp.exp(jnp.where(allowed, spread, -1e30))
            kernel = kernel + decay * products[i * tokens : (i + 1) * tokens, :]
            mixes.append((decay * scores).astype(BF16))
        gv_ref[:, at] = mm(jnp.concatenate(mixes, axis=1), split_g)
    kernel = kernel / state
    gbc_ref[:, :state] = mm(kernel.astype(BF16), c)
    gbc_ref[:, state:] = mm(kernel.T.astype(BF16), b)


def end_kernel(
    seq_total, len_ref, turned_ref, got_ref, sel_ref, gv_ref, gbc_ref, bc_ref, dec_ref, proj_ref, hid_ref,
    out_ref, hidden_ref, term_ref,
):
    tokens, state = bc_ref.shape[0], bc_ref.shape[1] // 2
    lead = (lax.axis_index("ctx") == 0).astype(F32)
    _, columns = prefix_sums(dec_ref)
    _, out_w = out_weights(columns, len_ref, lax.axis_index("ctx") * tokens)
    out_w = out_w * lead
    low = lax.broadcasted_iota(jnp.int32, (tokens, 128), 1) < 64
    edge = jnp.zeros((tokens, state), F32)
    b, side = bc_ref[:, :state], turned_ref[...]
    scale = lead / state + (1.0 - lead)
    for p in range(got_ref.shape[1] // 128):
        at = slice(128 * p, 128 * p + 128)
        got = (mm(side, got_ref[:, at]) * scale).astype(BF16)
        edge = edge + mm(sel_ref[:, at], got, NT)
        more = mm(b, got) * spread_pair(out_w, 2 * p, low)
        out_ref[:, at] = (gv_ref[:, at] + more).astype(BF16)
    gb = (gbc_ref[:, :state] + edge * lead).astype(BF16)
    gc = (gbc_ref[:, state:] + edge * ((1.0 - lead) / state)).astype(BF16)
    gbc = jnp.concatenate([gb, gc], axis=1)
    hidden_ref[...] = mm(gbc, proj_ref[...], NT).astype(BF16)
    turned = hid_ref[...].astype(F32).T.astype(BF16)
    term_ref[...] = (mm(turned, gbc) / seq_total).astype(BF16)


def call(body, name, flops, outs, *args):
    shapes = tuple(jax.ShapeDtypeStruct(s, d) for s, d in outs)
    return pl.pallas_call(
        body,
        out_shape=shapes,
        in_specs=[SM] + [VM] * (len(args) - 1),
        out_specs=tuple(VM for _ in shapes),
        cost_estimate=pl.CostEstimate(flops=flops, bytes_accessed=4000000, transcendentals=0),
        name=name,
    )(*args)


def paired(hidden_in, values, log_decay, doc_lengths, proj_bc, grad_out):
    n = lax.axis_size("fsdp")
    hid, val, dec, grad = hidden_in[0], values[0], log_decay[0], grad_out[0]
    tokens, inner = val.shape
    wide = proj_bc.shape[1]
    swap = [(0, 1), (1, 0)]
    (sel,) = call(
        weigh_kernel, "weigh", 10000000, [((tokens, inner), BF16)], doc_lengths, val, grad, dec
    )
    sel, proj_bc = lax.optimization_barrier((sel, proj_bc))
    got = lax.ppermute(sel, "ctx", swap)
    proj = gather(proj_bc, n)
    bc, side = call(
        project_kernel, "project", 200000000,
        [((tokens, wide), BF16), ((wide // 2, tokens), BF16)],
        doc_lengths, hid, proj,
    )
    turned = lax.ppermute(side, "ctx", swap)
    gv, gbc = call(
        middle_kernel, "middle", 4000000000,
        [((tokens, inner), F32), ((tokens, wide), F32)],
        doc_lengths, bc, val, grad, dec,
    )
    out, hidden, term = call(
        functools.partial(end_kernel, n * hidden_in.shape[0]), "end", 400000000,
        [((tokens, inner), BF16), (hid.shape, BF16), ((hid.shape[1], wide), BF16)],
        doc_lengths, turned, got, sel, gv, gbc, bc, dec, proj, hid,
    )
    return (out[None], hidden[None], scatter_sum(term, n))


def entering(value, axis, combine, identity, reverse):
    length, mine = (lax.axis_size(axis), lax.axis_index(axis))
    everything = jax.tree.map(
        lambda part, kind: lax.all_gather(part.astype(kind), axis),
        value,
        (jnp.bfloat16, jnp.bfloat16),
    )
    start = jax.tree.map(
        lambda part, zero: jnp.broadcast_to(jnp.asarray(zero, part.dtype), part.shape),
        value,
        identity,
    )

    def turn(k, before):
        at = length - 1 - k if reverse else k
        reached = at > mine if reverse else at < mine
        new = combine(
            before, jax.tree.map(lambda part, own: part[at].astype(own.dtype), everything, value)
        )
        return jax.tree.map(lambda a, b: jnp.where(reached, a, b), new, before)

    return lax.fori_loop(0, length, turn, start)


def combine_pairs(first_pair, second_pair):
    first_decay, first_state = first_pair
    second_decay, second_state = second_pair
    rows_count = first_state.shape[0]
    head_count = first_decay.shape[0]
    decayed = (
        first_state.reshape(rows_count, head_count, -1) * second_decay[None, :, None]
    ).reshape(first_state.shape)
    return (first_decay * second_decay, decayed + second_state)


def block_terms(b_rows, c_rows, value_rows, grad_rows, decay_rows, doc_ids, prev_doc):
    token_count, state_size = b_rows.shape
    head_count = decay_rows.shape[0]
    inner_width = value_rows.shape[1]
    head_dim = inner_width // head_count
    cumulative = jnp.cumsum(decay_rows, axis=1)
    last_doc = doc_ids[-1]
    token_places = jnp.arange(token_count, dtype=jnp.int32)
    allowed = (doc_ids[:, None] == doc_ids[None, :]) & (
        token_places[:, None] >= token_places[None, :]
    )
    spread = cumulative[:, :, None] - cumulative[:, None, :]
    decay_matrix = jnp.where(allowed[None], jnp.exp(jnp.where(allowed[None], spread, 0.0)), 0.0)
    in_weight = jnp.exp(cumulative) * (doc_ids == prev_doc).astype(jnp.float32)[None, :]
    out_weight = (
        jnp.exp(cumulative[:, -1:] - cumulative)
        * (doc_ids == last_doc).astype(jnp.float32)[None, :]
    )
    total_decay = jnp.exp(cumulative[:, -1]) * (last_doc == prev_doc).astype(jnp.float32)
    contract_last = (((1,), (1,)), ((), ()))
    scores = (
        lax.dot_general(c_rows, b_rows, contract_last, preferred_element_type=jnp.float32)
        / state_size
    )
    mixing = (decay_matrix * scores[None]).astype(jnp.bfloat16)
    value_heads = value_rows.reshape(token_count, head_count, head_dim)
    grad_heads = grad_rows.reshape(token_count, head_count, head_dim)
    products = jnp.einsum(
        "rhp,thp->hrt", grad_heads, value_heads, preferred_element_type=jnp.float32
    )
    kernel = (jnp.sum(decay_matrix * products, axis=0) / state_size).astype(jnp.bfloat16)
    grad_value_local = jnp.einsum(
        "hrt,rhp->thp", mixing, grad_heads, preferred_element_type=jnp.float32
    ).reshape(token_count, inner_width)
    contract_first = (((0,), (0,)), ((), ()))
    grad_b_local = lax.dot_general(
        kernel, c_rows, contract_first, preferred_element_type=jnp.float32
    )
    grad_c_local = jnp.dot(kernel, b_rows, preferred_element_type=jnp.float32)
    weighted_values = (
        (out_weight.T[:, :, None] * value_heads)
        .reshape(token_count, inner_width)
        .astype(jnp.bfloat16)
    )
    weighted_grads = (
        (in_weight.T[:, :, None] * grad_heads)
        .reshape(token_count, inner_width)
        .astype(jnp.bfloat16)
    )
    local_state = lax.dot_general(
        b_rows, weighted_values, contract_first, preferred_element_type=jnp.float32
    )
    local_grad = (
        lax.dot_general(c_rows, weighted_grads, contract_first, preferred_element_type=jnp.float32)
        / state_size
    )
    return (
        total_decay,
        local_state,
        local_grad,
        out_weight,
        weighted_values,
        weighted_grads,
        grad_value_local,
        grad_b_local,
        grad_c_local,
    )


def block_finish(b_rows, terms, state_in, grad_after):
    out_weight = terms[3]
    weighted_values = terms[4]
    weighted_grads = terms[5]
    grad_value_local = terms[6]
    grad_b_local = terms[7]
    grad_c_local = terms[8]
    token_count, state_size = b_rows.shape
    head_count = out_weight.shape[0]
    inner_width = weighted_values.shape[1]
    state_used = state_in.astype(jnp.bfloat16)
    grad_used = grad_after.astype(jnp.bfloat16)
    contract_last = (((1,), (1,)), ((), ()))
    grad_c_edge = (
        lax.dot_general(
            weighted_grads, state_used, contract_last, preferred_element_type=jnp.float32
        )
        / state_size
    )
    grad_b_edge = lax.dot_general(
        weighted_values, grad_used, contract_last, preferred_element_type=jnp.float32
    )
    edge_values = jnp.dot(b_rows, grad_used, preferred_element_type=jnp.float32).reshape(
        token_count, head_count, -1
    )
    grad_value_edge = (out_weight.T[:, :, None] * edge_values).reshape(token_count, inner_width)
    grad_values = (grad_value_local + grad_value_edge).astype(jnp.bfloat16)
    grad_bc = jnp.concatenate(
        [grad_b_local + grad_b_edge, grad_c_local + grad_c_edge], axis=1
    ).astype(jnp.bfloat16)
    return (grad_values, grad_bc)


def local(hidden_in, values, log_decay, doc_lengths, proj_bc, grad_out):
    token_count = hidden_in.shape[1]
    state_size = proj_bc.shape[1] // 2
    hidden_rows = hidden_in[0]
    first_proj = lax.all_gather(proj_bc, "fsdp", axis=0, tiled=True)
    projected = jnp.dot(hidden_rows, first_proj, preferred_element_type=jnp.float32).astype(
        jnp.bfloat16
    )
    b_rows = projected[:, :state_size]
    c_rows = projected[:, state_size:]
    lengths = doc_lengths[0]
    doc_starts = jnp.cumsum(lengths) - lengths
    first_token = lax.axis_index("ctx") * token_count
    token_places = first_token + jnp.arange(token_count, dtype=jnp.int32)
    doc_ids = jnp.sum((doc_starts[None, :] <= token_places[:, None]).astype(jnp.int32), axis=1)
    prev_doc = jnp.sum((doc_starts <= first_token - 1).astype(jnp.int32))
    terms = block_terms(b_rows, c_rows, values[0], grad_out[0], log_decay[0], doc_ids, prev_doc)
    total_decay = terms[0]
    unit_pair = (jnp.ones_like(total_decay), jnp.zeros_like(terms[1]))
    state_in = entering((total_decay, terms[1]), "ctx", combine_pairs, unit_pair, False)[1]
    grad_after = entering((total_decay, terms[2]), "ctx", combine_pairs, unit_pair, True)[1]
    grad_values, grad_bc = block_finish(b_rows, terms, state_in, grad_after)
    contract_last = (((1,), (1,)), ((), ()))
    grad_hidden = lax.dot_general(
        grad_bc, first_proj, contract_last, preferred_element_type=jnp.float32
    ).astype(jnp.bfloat16)
    seq_total = lax.axis_size("fsdp") * hidden_in.shape[0]
    contract_first = (((0,), (0,)), ((), ()))
    full_term = (
        lax.dot_general(hidden_rows, grad_bc, contract_first, preferred_element_type=jnp.float32)
        / seq_total
    )
    summed = lax.psum(full_term, "ctx")
    grad_proj = lax.psum_scatter(summed, "fsdp", scatter_dimension=0, tiled=True)
    return (grad_values[None], grad_hidden[None], grad_proj)


def solution(mesh):
    in_specs = (
        P("fsdp", "ctx", None),
        P("fsdp", "ctx", None),
        P("fsdp", None, "ctx"),
        P("fsdp", None),
        P("fsdp", None),
        P("fsdp", "ctx", None),
    )
    out_specs = (P("fsdp", "ctx", None), P("fsdp", "ctx", None), P("fsdp", None))
    body = paired if mesh.shape["ctx"] == 2 and mesh.shape["fsdp"] % 2 == 0 else local
    return jax.shard_map(body, mesh=mesh, in_specs=in_specs, out_specs=out_specs, check_vma=False)
```
